512 devices in a mesh: grp: 16 (over z_hi, y, core), seq: 32 (over z_lo, x).
Axes of the slice: x: 4, y: 4, z: 16 (z_hi: 2, z_lo: 8; z = z_hi * 8 + z_lo), core: 2. Of those that a mesh axis runs over, the one named last changes fastest.
Arguments:
- gate_out: bfloat16 [65536, 2048], P(('grp', 'seq')), may hold values from -6 to 6
- gate_in: bfloat16 [65536, 2048], P(('grp', 'seq')), may hold values from -6 to 6
- hyena_v: bfloat16 [65536, 2048], P(('grp', 'seq')), may hold values from -6 to 6
- queries: bfloat16 [65536, 2048], P(('grp', 'seq')), may hold values from -8 to 8
- attn_keys: bfloat16 [65536, 2048], P(('grp', 'seq')), may hold values from -8 to 8
- long_filter: float32 [128, 2048], replicated, may hold values from -0.5 to 0.5
Outputs:
- hyena_out: bfloat16 [65536, 2048], P(('grp', 'seq'))
- attended: bfloat16 [65536, 2048], P(('grp', 'seq'))
The draws below stay inside these ranges and needn't reach their ends.
All inputs are finite; a program needn't handle non-finite values.
Results may differ from the reference program's by a relative error of at most 0.0075.
The reference program's roundings to bfloat16 on the way (of `product`, `query_rot`, `key_rot` and `rounded`) count: a program that leaves them out, or rounds other values in their place, can miss the bound.
Values may be sent and summed in bfloat16 or wider, within the bound.
No kernel may reach another device: no remote copies, remote signals or barrier semaphores. Data moves between devices by JAX's collectives and lax.ppermute only.
A program may use at most 128 MiB of HBM per device.

```python
import math
import jax
import jax.numpy as jnp
from jax import lax

HEADS = 16
HEAD_DIM = 128
KTAP = 128
REACH = 11
TOK_DEV = 128
CHANNELS = 2048
TOKENS = 65536


def query_key_pair(key):
    feat_width = HEADS * HEAD_DIM
    query_out = jnp.clip(1.5 * jax.random.normal(jax.random.fold_in(key, 11), (TOKENS, feat_width), jnp.float32), -8.0, 8.0)
    key_out = jnp.clip(1.5 * jax.random.normal(jax.random.fold_in(key, 12), (TOKENS, feat_width), jnp.float32), -8.0, 8.0)
    return (query_out, key_out)


def draw_queries(key, part):
    return query_key_pair(key)[0].astype(jnp.bfloat16)


def draw_attn_keys(key, part):
    return query_key_pair(key)[1].astype(jnp.bfloat16)


def steps_of(stream_key, shape, pieces, low, top_value):
    def one(dim, shards_of):
        draws = jax.random.uniform(jax.random.fold_in(jax.random.fold_in(stream_key, 6), dim), (shards_of,), jnp.float32, low / len(pieces), top_value / len(pieces))
        return jnp.repeat(jnp.exp(draws), shape[dim] // shards_of).reshape((-1,) + (1,) * (len(shape) - dim - 1))

    level = one(*pieces[0])
    for cut in pieces[1:]:
        level = level * one(*cut)
    return level


def noise(own_key, dims, spread, bound, shards=(), held_as=jnp.bfloat16):
    loudness = steps_of(own_key, dims, shards, -0.22, 0.18) if shards else 1.0
    values = jax.random.normal(own_key, dims, jnp.float32) * spread * loudness
    return jnp.minimum(jnp.maximum(values, -bound), bound).astype(held_as)


def setup_inputs(seed: int = 0) -> dict:
    arg_keys = jax.random.split(jax.random.key(seed), 7)
    return {
        "gate_out": noise(arg_keys[0], (TOKENS, CHANNELS), 1.0, 6.0, ((0, 512),)),
        "gate_in": noise(arg_keys[1], (TOKENS, CHANNELS), 1.0, 6.0, ((0, 512),)),
        "hyena_v": noise(arg_keys[2], (TOKENS, CHANNELS), 1.0, 6.0, ((0, 512),)),
        "queries": draw_queries(jax.random.fold_in(arg_keys[6], 71), 0),
        "attn_keys": draw_attn_keys(jax.random.fold_in(arg_keys[6], 71), 0),
        "long_filter": noise(arg_keys[5], (KTAP, CHANNELS), KTAP ** -0.5, 0.5, (), jnp.float32),
    }


rope_base = 10000.0
rope_stretch = 128.0
mask_fill = -1e+30

def rotate(values, positions, head_count):
    row_total = values.shape[0]
    feat_width = values.shape[1]
    head_dim = feat_width // head_count
    half_dim = head_dim // 2
    pair_index = jnp.arange(half_dim).astype(jnp.float32)
    frequency = jnp.exp(pair_index * (-2.0 * math.log(rope_base) / head_dim)) / rope_stretch
    angles = positions.astype(jnp.float32)[:, None] * frequency[None, :]
    cosine = jnp.cos(angles)[:, None, :]
    sine_part = jnp.sin(angles)[:, None, :]
    split_rows = values.astype(jnp.float32).reshape(row_total, head_count, head_dim)
    lower_half = split_rows[..., :half_dim]
    upper_half = split_rows[..., half_dim:]
    rotated = jnp.concatenate([lower_half * cosine - upper_half * sine_part, upper_half * cosine + lower_half * sine_part], axis=2)
    return rotated.reshape(row_total, feat_width).astype(jnp.bfloat16)

def apply_filter(window, taps):
    tap_count = taps.shape[0]
    row_total = window.shape[0] - tap_count + 1
    running = jnp.zeros((row_total, window.shape[1]), jnp.float32)
    for offset in range(tap_count):
        begin_row = tap_count - 1 - offset
        running = running + taps[offset][None, :] * window[begin_row:begin_row + row_total].astype(jnp.float32)
    return running

def reference(gate_out, gate_in, hyena_v, queries, attn_keys, long_filter):
    tokens_all, feat_width = gate_out.shape
    head_dim = feat_width // HEADS
    product = (gate_in.astype(jnp.float32) * hyena_v.astype(jnp.float32)).astype(jnp.bfloat16)
    padded = jnp.concatenate([jnp.zeros((KTAP - 1, feat_width), jnp.bfloat16), product], axis=0)
    block_ids = jnp.arange(tokens_all // TOK_DEV, dtype=jnp.int32)

    def filter_rows(block_index):
        window = lax.dynamic_slice_in_dim(padded, (block_index * TOK_DEV).astype(jnp.int32), TOK_DEV + KTAP - 1, 0)
        return apply_filter(window, long_filter)
    filtered = lax.map(filter_rows, block_ids).reshape(tokens_all, feat_width)
    hyena_out = (gate_out.astype(jnp.float32) * filtered).astype(jnp.bfloat16)
    positions = jnp.arange(tokens_all, dtype=jnp.int32)
    query_rot = rotate(queries, positions, HEADS)
    key_rot = rotate(attn_keys, positions, HEADS)
    reach_rows = REACH * TOK_DEV
    key_pad = jnp.concatenate([jnp.zeros((reach_rows, feat_width), jnp.bfloat16), key_rot], axis=0)
    value_pad = jnp.concatenate([jnp.zeros((reach_rows, feat_width), jnp.bfloat16), hyena_out], axis=0)
    score_scale = 1.0 / math.sqrt(head_dim)

    def attend(block_index):
        row_start = (block_index * TOK_DEV).astype(jnp.int32)
        query_blk = lax.dynamic_slice_in_dim(query_rot, row_start, TOK_DEV, 0)
        key_blk = lax.dynamic_slice_in_dim(key_pad, row_start, reach_rows + TOK_DEV, 0)
        value_blk = lax.dynamic_slice_in_dim(value_pad, row_start, reach_rows + TOK_DEV, 0)
        query_pos = row_start + jnp.arange(TOK_DEV, dtype=jnp.int32)
        key_pos = row_start - reach_rows + jnp.arange(reach_rows + TOK_DEV, dtype=jnp.int32)
        query_heads = query_blk.astype(jnp.float32).reshape(TOK_DEV, HEADS, head_dim)
        key_heads = key_blk.astype(jnp.float32).reshape(reach_rows + TOK_DEV, HEADS, head_dim)
        scores = jnp.einsum('qhd,khd->hqk', query_heads, key_heads) * score_scale
        distance = query_pos[:, None] - key_pos[None, :]
        allowed = (distance >= 0) & (distance < reach_rows) & (key_pos >= 0)[None, :]
        scores = jnp.where(allowed[None, :, :], scores, mask_fill)
        highest = lax.optimization_barrier(jnp.max(scores, axis=2))
        weights = jnp.exp(scores - highest[:, :, None])
        totals = lax.optimization_barrier(jnp.sum(weights, axis=2))
        rounded = weights.astype(jnp.bfloat16)
        value_heads = value_blk.astype(jnp.float32).reshape(reach_rows + TOK_DEV, HEADS, head_dim)
        summed = jnp.einsum('hqk,khd->qhd', rounded.astype(jnp.float32), value_heads)
        result = summed / jnp.transpose(totals)[:, :, None]
        return result.reshape(TOK_DEV, feat_width).astype(jnp.bfloat16)
    attended = lax.map(attend, block_ids).reshape(tokens_all, feat_width)
    return (hyena_out, attended)
```

```python
import functools
import math

import jax
import jax.numpy as jnp
from jax import lax
from jax.experimental import pallas as pl
from jax.experimental.pallas import tpu as pltpu
from jax.sharding import PartitionSpec as P

HEADS = 16
REACH = 11
RING = 4
AXES = ("grp", "seq")

rope_base = 10000.0
rope_stretch = 128.0
mask_fill = -1e30

F32 = jnp.float32
BF16 = jnp.bfloat16


def shifted(x, by):
    devices = lax.axis_size(AXES)
    return lax.ppermute(x, AXES, [(i, i + by) for i in range(devices - by)])


def ring_exchange(x):
    spans = lax.axis_size("seq")
    groups = [[RING * g + i for i in range(RING)] for g in range(spans // RING)]
    return lax.all_to_all(x, "seq", 0, 0, axis_index_groups=groups, tiled=True)


def rope_tables(positions, head_dim):
    half_dim = head_dim // 2
    pair_index = jnp.arange(half_dim).astype(F32)
    frequency = jnp.exp(pair_index * (-2.0 * math.log(rope_base) / head_dim)) / rope_stretch
    angles = positions.astype(F32)[:, None] * frequency[None, :]
    cosine = jnp.cos(angles)
    sine = jnp.sin(angles)
    return (
        jnp.concatenate([cosine, cosine], axis=1),
        jnp.concatenate([-sine, sine], axis=1),
    )


def rope_kernel(x_ref, c_ref, s_ref, o_ref):
    cosine = c_ref[...]
    sine = s_ref[...]
    head_dim = cosine.shape[1]
    for h in range(x_ref.shape[1] // head_dim):
        cols = slice(h * head_dim, (h + 1) * head_dim)
        v = x_ref[:, cols].astype(F32)
        o_ref[0, :, cols] = (v * cosine + pltpu.roll(v, head_dim // 2, 1) * sine).astype(BF16)


def rope(x, tables):
    rows, feat = x.shape
    part = feat // RING
    hd = tables[0].shape[1]
    return pl.pallas_call(
        rope_kernel,
        grid=(RING,),
        in_specs=[
            pl.BlockSpec((rows, part), lambda i: (0, i)),
            pl.BlockSpec((rows, hd), lambda i: (0, 0)),
            pl.BlockSpec((rows, hd), lambda i: (0, 0)),
        ],
        out_specs=pl.BlockSpec((1, rows, part), lambda i: (i, 0, 0)),
        out_shape=jax.ShapeDtypeStruct((RING, rows, part), BF16),
        cost_estimate=pl.CostEstimate(
            flops=rows * feat * 4, bytes_accessed=rows * feat * 4, transcendentals=0
        ),
    )(x, *tables)


LANES = 128


def filter_kernel(rim_ref, product_ref, gate_ref, taps_ref, out_ref, parts_ref):
    rows = product_ref.shape[0]
    taps = taps_ref.shape[0]
    window = jnp.concatenate([rim_ref[...].astype(F32), product_ref[...].astype(F32)], axis=0)
    total = jnp.zeros((rows, LANES), F32)
    for r in range(8):
        moved = window if r == 0 else pltpu.roll(window, r, 0)
        for m in range(taps // 8):
            j = 8 * m + r
            total = total + taps_ref[j : j + 1, :] * moved[rows - 8 * m : 2 * rows - 8 * m, :]
    mixed = (gate_ref[...].astype(F32) * total).astype(BF16)
    out_ref[...] = mixed
    parts_ref[0] = mixed


def hyena(rim, product, gate_out, long_filter):
    rows, feat = product.shape
    per = feat // RING // LANES
    taps = long_filter.shape[0]
    col = lambda i: (0, i)
    return pl.pallas_call(
        filter_kernel,
        grid=(feat // LANES,),
        in_specs=[
            pl.BlockSpec((rows, LANES), col),
            pl.BlockSpec((rows, LANES), col),
            pl.BlockSpec((rows, LANES), col),
            pl.BlockSpec((taps, LANES), col),
        ],
        out_specs=[
            pl.BlockSpec((rows, LANES), col),
            pl.BlockSpec((1, rows, LANES), lambda i: (i // per, 0, i % per)),
        ],
        out_shape=[
            jax.ShapeDtypeStruct((rows, feat), BF16),
            jax.ShapeDtypeStruct((RING, rows, feat // RING), BF16),
        ],
        cost_estimate=pl.CostEstimate(
            flops=rows * feat * taps * 2, bytes_accessed=rows * feat * 14, transcendentals=0
        ),
    )(rim, product, gate_out, long_filter)


def level_kernel(back, first, last, scale, level_ref, q_ref, k_ref, v_ref, *rest):
    rest = list(rest)
    if not first:
        acc_in, top_in, tot_in = rest[:3]
        rest = rest[3:]
    if last:
        (o_ref,) = rest
    else:
        acc_out, top_out, tot_out = rest
    tok = q_ref.shape[1]
    hd = q_ref.shape[2]
    k_base = RING - k_ref.shape[0]
    v_base = RING - v_ref.shape[0]
    q_off = lax.broadcasted_iota(jnp.int32, (tok, tok), 0)
    k_off = lax.broadcasted_iota(jnp.int32, (tok, tok), 1)

    def finish(qb, acc, tot):
        o_ref[qb] = (acc / tot).astype(BF16)

    def pass_on(qb):
        rows = slice(qb * tok, (qb + 1) * tok)
        if last:
            finish(qb, acc_in[rows, :], tot_in[rows, :])
        else:
            acc_out[rows, :] = acc_in[rows, :]
            top_out[rows, :] = top_in[rows, :]
            tot_out[rows, :] = tot_in[rows, :]

    def work(qb):
        lo = max(0, back * RING + qb - REACH)
        hi = min(RING - 1, back * RING + qb)
        if lo > hi:
            pass_on(qb)
            return
        rows = slice(qb * tok, (qb + 1) * tok)
        span = hi - lo + 1
        keys = k_ref[lo - k_base : hi + 1 - k_base].reshape(span * tok, hd)
        vals = v_ref[lo - v_base : hi + 1 - v_base].reshape(span * tok, hd)
        s = lax.dot_general(
            q_ref[qb], keys, (((1,), (1,)), ((), ())), preferred_element_type=F32
        )
        if back * RING + qb - lo == REACH:
            head = jnp.where(k_off > q_off, s[:, :tok], mask_fill)
            s = head if span == 1 else jnp.concatenate([head, s[:, tok:]], axis=1)
        if back * RING + qb - hi == 0:
            tail = jnp.where(k_off <= q_off, s[:, -tok:], mask_fill)
            s = tail if span == 1 else jnp.concatenate([s[:, :-tok], tail], axis=1)
        top = jnp.max(s, axis=1, keepdims=True)
        if not first:
            top = jnp.maximum(top_in[rows, 0:1], top)
        w = jnp.exp((s - top) * scale)
        tot = jnp.sum(w, axis=1, keepdims=True)
        acc = jnp.dot(w.astype(BF16), vals, preferred_element_type=F32)
        if not first:
            factor = jnp.exp((top_in[rows, 0:1] - top) * scale)
            tot = tot + tot_in[rows, 0:1] * factor
            acc = acc + acc_in[rows, :] * factor
        if last:
            finish(qb, acc, tot)
        else:
            acc_out[rows, :] = acc
            top_out[rows, :] = jnp.broadcast_to(top, (tok, hd))
            tot_out[rows, :] = jnp.broadcast_to(tot, (tok, hd))

    if first:
        for qb in range(RING):
            work(qb)
    else:

        @pl.when(level_ref[0] >= back)
        def _():
            for qb in range(RING):
                work(qb)

        @pl.when(level_ref[0] < back)
        def _():
            for qb in range(RING):
                pass_on(qb)


def level_step(back, last, level, q, k, v, carry):
    first = carry is None
    parts, tok, width = q.shape
    hd = 128
    heads = width // hd
    blk = lambda n: pl.BlockSpec((n, tok, hd), lambda h, _: (0, 0, h))
    state = pl.BlockSpec((parts * tok, hd), lambda h, _: (0, h))
    state_shape = jax.ShapeDtypeStruct((parts * tok, width), F32)
    if last:
        out_specs, out_shape = blk(parts), jax.ShapeDtypeStruct(q.shape, BF16)
    else:
        out_specs, out_shape = [state] * 3, [state_shape] * 3
    args = [] if first else list(carry)
    pairs = parts * parts * tok * tok * heads
    return pl.pallas_call(
        functools.partial(level_kernel, back, first, last, 1.0 / math.sqrt(hd)),
        grid_spec=pltpu.PrefetchScalarGridSpec(
            num_scalar_prefetch=1,
            grid=(heads,),
            in_specs=[blk(parts), blk(k.shape[0]), blk(v.shape[0])] + [state] * len(args),
            out_specs=out_specs,
        ),
        out_shape=out_shape,
        cost_estimate=pl.CostEstimate(
            flops=pairs * hd * 4, bytes_accessed=8 * 1024 * 1024, transcendentals=pairs
        ),
    )(level, q, k, v, *args)


def local(gate_out, gate_in, hyena_v, queries, attn_keys, long_filter):
    rows, feat = gate_out.shape
    head_dim = feat // HEADS
    device = lax.axis_index(AXES)
    positions = device * rows + jnp.arange(rows, dtype=jnp.int32)
    level = (device // RING).astype(jnp.int32).reshape(1)
    product = (gate_in.astype(F32) * hyena_v.astype(F32)).astype(BF16)
    rim = shifted(product, 1)
    tables = rope_tables(positions, head_dim)
    key_own = rope(attn_keys, tables)
    key_raw1 = shifted(key_own, RING)
    key_raw2 = shifted(key_raw1, RING)
    key_raw3 = shifted(key_raw2, RING)
    query = rope(queries, tables)
    hyena_out, value_own = hyena(rim, product, gate_out, long_filter)

    k0 = ring_exchange(key_own)
    q = ring_exchange(query)
    v0 = ring_exchange(value_own)
    v1 = shifted(v0, RING)
    v2 = shifted(v1, RING)
    v3 = shifted(v2[1:], RING)
    k1 = ring_exchange(key_raw1)
    k2 = ring_exchange(key_raw2)
    k3 = ring_exchange(key_raw3)

    carry = level_step(0, False, level, q, k0, v0, None)
    carry = level_step(1, False, level, q, k1, v1, carry)
    carry = level_step(2, False, level, q, k2, v2, carry)
    out = level_step(3, True, level, q, k3, v3, carry)
    back = ring_exchange(out)
    attended = jnp.transpose(back, (1, 0, 2)).reshape(rows, feat)
    return (hyena_out, attended)


def solution(mesh):
    rows = P(AXES, None)
    return jax.shard_map(
        local,
        mesh=mesh,
        in_specs=(rows,) * 5 + (P(),),
        out_specs=(rows, rows),
        check_vma=False,
    )
```

```python
import functools
import math

import jax
import jax.numpy as jnp
import ml_dtypes
import numpy as np
from jax import lax
from jax.experimental import pallas as pl
from jax.experimental.pallas import tpu as pltpu
from jax.sharding import PartitionSpec as P

HEADS = 16
REACH = 11
RING = 4
AXES = ("grp", "seq")

rope_base = 10000.0
rope_stretch = 128.0
mask_fill = -1e30

F32 = jnp.float32
BF16 = jnp.bfloat16


def shifted(x, by):
    devices = lax.axis_size(AXES)
    return lax.ppermute(x, AXES, [(i, i + by) for i in range(devices - by)])


def ring_exchange(x):
    spans = lax.axis_size("seq")
    groups = [[RING * g + i for i in range(RING)] for g in range(spans // RING)]
    return lax.all_to_all(x, "seq", 0, 0, axis_index_groups=groups, tiled=True)


def rope_tables(positions, head_dim):
    half_dim = head_dim // 2
    pair_index = jnp.arange(half_dim).astype(F32)
    frequency = jnp.exp(pair_index * (-2.0 * math.log(rope_base) / head_dim)) / rope_stretch
    angles = positions.astype(F32)[:, None] * frequency[None, :]
    cosine = jnp.cos(angles)
    sine = jnp.sin(angles)
    return (
        jnp.concatenate([cosine, cosine], axis=1),
        jnp.concatenate([-sine, sine], axis=1),
    )


HELD = pl.BlockSpec(memory_space=pltpu.VMEM)


def prep_kernel(gate_in_ref, value_ref, gate_ref, p_ref, g_ref):
    part = p_ref.shape[2]
    for i in range(RING):
        cols = slice(i * part, (i + 1) * part)
        p_ref[i] = (gate_in_ref[:, cols].astype(F32) * value_ref[:, cols].astype(F32)).astype(BF16)
        g_ref[i] = gate_ref[:, cols]


def prep(gate_in, hyena_v, gate_out):
    rows, feat = gate_in.shape
    part = feat // RING
    shape = jax.ShapeDtypeStruct((RING, rows, part), BF16)
    return pl.pallas_call(
        prep_kernel,
        in_specs=[HELD] * 3,
        out_specs=[HELD] * 2,
        out_shape=[shape] * 2,
        cost_estimate=pl.CostEstimate(
            flops=rows * feat, bytes_accessed=rows * feat * 10, transcendentals=0
        ),
    )(gate_in, hyena_v, gate_out)


def rope_kernel(joined, x_ref, c_ref, s_ref, *rest):
    o_ref = rest[-1]
    cosine = c_ref[...]
    sine = s_ref[...]
    rows, head_dim = cosine.shape
    if joined:
        o_ref[:, :rows] = rest[0][...]
    base = rows if joined else 0
    per = o_ref.shape[2] // head_dim
    for h in range(x_ref.shape[1] // head_dim):
        v = x_ref[:, h * head_dim : (h + 1) * head_dim].astype(F32)
        turned = v * cosine + pltpu.roll(v, head_dim // 2, 1) * sine
        cols = slice(h % per * head_dim, (h % per + 1) * head_dim)
        o_ref[h // per, base : base + rows, cols] = turned.astype(BF16)


def rope(x, tables, before=None):
    rows, feat = x.shape
    part = feat // RING
    joined = before is not None
    out_rows = rows * 2 if joined else rows
    return pl.pallas_call(
        functools.partial(rope_kernel, joined),
        in_specs=[HELD] * (4 if joined else 3),
        out_specs=HELD,
        out_shape=jax.ShapeDtypeStruct((RING, out_rows, part), BF16),
        cost_estimate=pl.CostEstimate(
            flops=rows * feat * 4, bytes_accessed=rows * feat * 4, transcendentals=0
        ),
    )(x, *tables, *([before] if joined else []))


def halves(x):
    high = x.astype(BF16)
    return high, (x - high.astype(F32)).astype(BF16)


def fourier_tables(taps):
    size = 2 * taps
    f = np.arange(taps)[:, None]
    n = np.arange(size)[None, :]
    angle = 2.0 * np.pi * ((f * n) % size) / size
    cos_rows = np.cos(angle)
    sin_rows = np.sin(angle)
    sin_rows[0] = 1.0 - 2.0 * (n[0] % 2)
    forward = np.concatenate([cos_rows, sin_rows], axis=0)
    weight = np.full((taps, 1), 2.0 / size)
    weight[0] = 1.0 / size
    inverse = np.concatenate([cos_rows * weight, sin_rows * weight], axis=0)[:, taps:].T

    def split(m):
        m = m.astype(np.float32)
        high = m.astype(ml_dtypes.bfloat16)
        low = (m - high.astype(np.float32)).astype(ml_dtypes.bfloat16)
        return high, low

    fh, fl = split(forward)
    ih, il = split(inverse)
    both = np.concatenate([fh, fl], axis=0)
    taps_side = np.concatenate([fh[:, :taps], fh[:, :taps], fl[:, :taps]], axis=1)
    back = np.concatenate([ih, ih, il], axis=1)
    return jnp.asarray(both), jnp.asarray(taps_side), jnp.asarray(back)


def filter_kernel(where_ref, rim_ref, p_ref, g_ref, taps_ref, fwd_ref, tap_side_ref, inv_ref, o_ref, near_ref, far_ref):
    taps = taps_ref.shape[0]
    th, tl = halves(taps_ref[...])
    h = jnp.dot(
        tap_side_ref[...], jnp.concatenate([th, tl, th], axis=0), preferred_element_type=F32
    )
    hc, hs = h[:taps], h[taps:]
    lone = lax.broadcasted_iota(jnp.int32, hc.shape, 0) == 0
    cross_c = jnp.where(lone, 0.0, hs)
    main_s = jnp.where(lone, hs, hc)
    for b in range(RING):
        rim = rim_ref[0] if b == 0 else p_ref[b - 1]
        window = jnp.concatenate([rim, p_ref[b]], axis=0)
        x2 = jnp.dot(fwd_ref[...], window, preferred_element_type=F32)
        x = x2[: 2 * taps] + x2[2 * taps :]
        xc, xs = x[:taps], x[taps:]
        yc = xc * hc - xs * cross_c
        ys = xc * cross_c + xs * main_s
        yh, yl = halves(jnp.concatenate([yc, ys], axis=0))
        y = jnp.dot(
            inv_ref[...], jnp.concatenate([yh, yl, yh], axis=0), preferred_element_type=F32
        )
        mixed = (g_ref[b].astype(F32) * y).astype(BF16)
        o_ref[b] = mixed

        @pl.when(pl.program_id(0) == 0)
        def _():
            near_ref[b] = mixed

        @pl.when(pl.program_id(0) == 1)
        def _():
            far_ref[b] = mixed


def hyena(ring_place, rim, product, gate, long_filter):
    parts, rows, width = product.shape
    taps = long_filter.shape[0]
    lanes = width // 2
    per = 2
    tables = fourier_tables(taps)
    col = lambda n: pl.BlockSpec((n, rows, lanes), lambda i, _: (0, 0, i))
    whole = lambda t: pl.BlockSpec(t.shape, lambda i, _: (0, 0))
    return pl.pallas_call(
        filter_kernel,
        grid_spec=pltpu.PrefetchScalarGridSpec(
            num_scalar_prefetch=1,
            grid=(per,),
            in_specs=[col(1), col(parts), col(parts)]
            + [pl.BlockSpec((taps, lanes), lambda i, place: (0, place[0] * per + i))]
            + [whole(t) for t in tables],
            out_specs=[col(parts)]
            + [pl.BlockSpec((parts, rows, lanes), lambda i, _: (0, 0, 0))] * 2,
        ),
        out_shape=[jax.ShapeDtypeStruct(product.shape, BF16)]
        + [jax.ShapeDtypeStruct((parts, rows, lanes), BF16)] * 2,
        cost_estimate=pl.CostEstimate(
            flops=1_000_000_000, bytes_accessed=3 * 1024 * 1024, transcendentals=0
        ),
    )(ring_place, rim, product, gate, long_filter, *tables)


STRIPS = {
    0: ((0, 2, 0, 2, True), (2, 4, 0, 4, True)),
    1: ((0, 4, 0, 4, False),),
    2: ((0, 3, 0, 4, False), (3, 4, 0, 4, True)),
    3: ((0, 2, 1, 4, True), (2, 4, 3, 4, True)),
}
FAR = 3
HEAD_DIM = 128


def scores(back, h, strip, tok, kq_ref, k_ref):
    q0, q1, k0, k1, masked = strip
    lanes = slice(h * HEAD_DIM, (h + 1) * HEAD_DIM)
    keys = k_ref[k0:k1, :tok, lanes].reshape((k1 - k0) * tok, HEAD_DIM)
    qs = kq_ref[q0:q1, tok : 2 * tok, lanes].reshape((q1 - q0) * tok, HEAD_DIM)
    s = lax.dot_general(keys, qs, (((1,), (1,)), ((), ())), preferred_element_type=F32)
    if masked:
        gap = (back * RING + q0 - k0) * tok
        gap = gap + lax.broadcasted_iota(jnp.int32, s.shape, 1)
        gap = gap - lax.broadcasted_iota(jnp.int32, s.shape, 0)
        s = jnp.where(gap >= 0 if back == 0 else gap < REACH * tok, s, mask_fill)
    return s


def weigh(vals, w):
    return lax.dot_general(vals, w, (((0,), (0,)), ((), ())), preferred_element_type=F32)


def level_kernel(back, scale, level_ref, kq_ref, k_ref, near_ref, far_ref, *rest):
    first = back == 0
    if not first:
        acc_in, stat_in = rest[:2]
    acc_out, stat_out = rest[-2:]
    tok = near_ref.shape[1]
    heads = 2 * near_ref.shape[2] // HEAD_DIM

    def work(h, strip):
        q0, q1, k0, k1, _ = strip
        cols = slice(q0 * tok, q1 * tok)
        v_ref = near_ref if h < heads // 2 else far_ref
        hh = h % (heads // 2)
        vals = v_ref[k0:k1, :, hh * HEAD_DIM : (hh + 1) * HEAD_DIM]
        vals = vals.reshape((k1 - k0) * tok, HEAD_DIM)
        s = scores(back, h, strip, tok, kq_ref, k_ref)
        top = jnp.max(s, axis=0, keepdims=True)
        if not first:
            top = jnp.maximum(stat_in[h, 0:1, cols], top)
        w = jnp.exp((s - top) * scale)
        tot = jnp.sum(w, axis=0, keepdims=True)
        acc = weigh(vals, w.astype(BF16))
        if not first:
            factor = jnp.exp((stat_in[h, 0:1, cols] - top) * scale)
            tot = tot + stat_in[h, 1:2, cols] * factor
            acc = acc + acc_in[h, :, cols] * factor
        acc_out[h, :, cols] = acc
        stat_out[h, 0:1, cols] = top
        stat_out[h, 1:2, cols] = tot

    def all_work():
        for h in range(heads):
            for strip in STRIPS[back]:
                work(h, strip)

    if first:
        all_work()
    else:
        pl.when(level_ref[0] >= back)(all_work)

        @pl.when(level_ref[0] < back)
        def _():
            acc_out[...] = acc_in[...]
            stat_out[...] = stat_in[...]


def level_step(back, level, kq, k, v, carry):
    _, tok, half = v[0].shape
    heads = 2 * half // HEAD_DIM
    args = [] if carry is None else list(carry)
    pairs = RING * RING * tok * tok * heads
    return pl.pallas_call(
        functools.partial(level_kernel, back, 1.0 / math.sqrt(HEAD_DIM)),
        in_specs=[pl.BlockSpec(memory_space=pltpu.SMEM)] + [HELD] * (4 + len(args)),
        out_specs=[HELD] * 2,
        out_shape=[
            jax.ShapeDtypeStruct((heads, HEAD_DIM, RING * tok), F32),
            jax.ShapeDtypeStruct((heads, 8, RING * tok), F32),
        ],
        cost_estimate=pl.CostEstimate(
            flops=pairs * HEAD_DIM * 4, bytes_accessed=4 * 1024 * 1024, transcendentals=pairs
        ),
    )(level, kq, k, *v, *args)


def far_weights_kernel(scale, level_ref, kq_ref, k_ref, stat_in, *outs):
    w_refs, stat_out = outs[:-1], outs[-1]
    tok = k_ref.shape[1]
    heads = stat_in.shape[0]

    @pl.when(level_ref[0] >= FAR)
    def _():
        for h in range(heads):
            for w_ref, strip in zip(w_refs, STRIPS[FAR]):
                cols = slice(strip[0] * tok, strip[1] * tok)
                s = scores(FAR, h, strip, tok, kq_ref, k_ref)
                top = jnp.maximum(stat_in[h, 0:1, cols], jnp.max(s, axis=0, keepdims=True))
                w = jnp.exp((s - top) * scale)
                factor = jnp.exp((stat_in[h, 0:1, cols] - top) * scale)
                tot = stat_in[h, 1:2, cols] * factor + jnp.sum(w, axis=0, keepdims=True)
                w_ref[h] = w.astype(BF16)
                stat_out[h, 0:1, cols] = factor
                stat_out[h, 1:2, cols] = tot

    @pl.when(level_ref[0] < FAR)
    def _():
        for w_ref in w_refs:
            w_ref[...] = jnp.zeros_like(w_ref)
        for h in range(heads):
            stat_out[h, 0:1] = jnp.ones_like(stat_in[h, 0:1])
            stat_out[h, 1:2] = stat_in[h, 1:2]


def far_weights(level, kq, k, stat):
    heads = stat.shape[0]
    tok = k.shape[1]
    sizes = [((k1 - k0) * tok, (q1 - q0) * tok) for q0, q1, k0, k1, _ in STRIPS[FAR]]
    pairs = sum(a * b for a, b in sizes) * heads
    return pl.pallas_call(
        functools.partial(far_weights_kernel, 1.0 / math.sqrt(HEAD_DIM)),
        in_specs=[pl.BlockSpec(memory_space=pltpu.SMEM)] + [HELD] * 3,
        out_specs=[HELD] * (len(sizes) + 1),
        out_shape=[jax.ShapeDtypeStruct((heads,) + size, BF16) for size in sizes]
        + [jax.ShapeDtypeStruct(stat.shape, F32)],
        cost_estimate=pl.CostEstimate(
            flops=pairs * HEAD_DIM * 2, bytes_accessed=2 * 1024 * 1024, transcendentals=pairs
        ),
    )(level, kq, k, stat)


def finish_kernel(h0, acc_ref, v_ref, *rest):
    w_refs, stat_ref, o_ref = rest[:-2], rest[-2], rest[-1]
    blocks, tok, half = v_ref.shape
    base = RING - blocks
    for hh in range(half // HEAD_DIM):
        h = h0 + hh
        lanes = slice(hh * HEAD_DIM, (hh + 1) * HEAD_DIM)
        for w_ref, (q0, q1, k0, k1, _) in zip(w_refs, STRIPS[FAR]):
            cols = slice(q0 * tok, q1 * tok)
            vals = v_ref[k0 - base : k1 - base, :, lanes].reshape((k1 - k0) * tok, HEAD_DIM)
            acc = acc_ref[h, :, cols] * stat_ref[h, 0:1, cols] + weigh(vals, w_ref[h])
            done = acc / stat_ref[h, 1:2, cols]
            for qb in range(q0, q1):
                piece = done[:, (qb - q0) * tok : (qb - q0 + 1) * tok]
                o_ref[qb, :, lanes] = jnp.transpose(piece).astype(BF16)


def finish(h0, acc, v, weights):
    _, tok, half = v.shape
    return pl.pallas_call(
        functools.partial(finish_kernel, h0),
        in_specs=[HELD] * (2 + len(weights)),
        out_specs=HELD,
        out_shape=jax.ShapeDtypeStruct((RING, tok, half), BF16),
        cost_estimate=pl.CostEstimate(
            flops=200_000_000, bytes_accessed=2 * 1024 * 1024, transcendentals=0
        ),
    )(acc, v, *weights)


def join_kernel(*refs):
    o_ref = refs[-1]
    at = 0
    for j in range(RING):
        for ref in refs[:-1]:
            width = ref.shape[2]
            o_ref[:, at : at + width] = ref[j]
            at += width


def join(*pieces):
    _, rows, _ = pieces[0].shape
    feat = RING * sum(p.shape[2] for p in pieces)
    return pl.pallas_call(
        join_kernel,
        in_specs=[HELD] * len(pieces),
        out_shape=jax.ShapeDtypeStruct((rows, feat), BF16),
        cost_estimate=pl.CostEstimate(
            flops=0, bytes_accessed=rows * feat * 4, transcendentals=0
        ),
    )(*pieces)


def local(gate_out, gate_in, hyena_v, queries, attn_keys, long_filter):
    rows, feat = gate_out.shape
    head_dim = feat // HEADS
    device = lax.axis_index(AXES).astype(jnp.int32)
    positions = device * rows + jnp.arange(rows, dtype=jnp.int32)
    level = lax.shift_right_logical(device, 2).reshape(1)
    place = lax.bitwise_and(device, 3).reshape(1)
    product4, gate4 = prep(gate_in, hyena_v, gate_out)
    product = ring_exchange(product4)
    tables = rope_tables(positions, head_dim)
    key_own = rope(attn_keys, tables)
    key_raw1 = shifted(key_own, RING)
    rim = shifted(product[RING - 1 :], RING)
    gate = ring_exchange(gate4)
    kq_own = rope(queries, tables, key_own)
    kq = ring_exchange(kq_own)
    key_raw2 = shifted(key_raw1, RING)
    v0, v0a, v0b = hyena(place, rim, product, gate, long_filter)
    v1a = shifted(v0a, RING)
    v1b = shifted(v0b, RING)
    k1 = ring_exchange(key_raw1)
    key_raw3 = shifted(key_raw2, RING)
    k2 = ring_exchange(key_raw2)
    carry = level_step(0, level, kq, kq, (v0a, v0b), None)
    v2a = shifted(v1a, RING)
    v2b = shifted(v1b, RING)
    carry = level_step(1, level, kq, k1, (v1a, v1b), carry)
    back_h = ring_exchange(v0)
    k3 = ring_exchange(key_raw3)
    v3a = shifted(v2a[1:], RING)
    v3b = shifted(v2b[1:], RING)
    hyena_out = join(back_h)
    acc, stat = level_step(2, level, kq, k2, (v2a, v2b), carry)
    weights = far_weights(level, kq, k3, stat)
    out_a = finish(0, acc, v3a, weights)
    back_a = ring_exchange(out_a)
    out_b = finish(acc.shape[0] // 2, acc, v3b, weights)
    back_b = ring_exchange(out_b)
    attended = join(back_a, back_b)
    return (hyena_out, attended)


def solution(mesh):
    rows = P(AXES, None)
    return jax.shard_map(
        local,
        mesh=mesh,
        in_specs=(rows,) * 5 + (P(),),
        out_specs=(rows, rows),
        check_vma=False,
    )
```
